256 devices in a mesh: dp: 4 (over x_lo, core), expert: 64 (over z, x_hi, y).
Axes of the slice: x: 4 (x_hi: 2, x_lo: 2; x = x_hi * 2 + x_lo), y: 4, z: 8, core: 2. Of those that a mesh axis runs over, the one named last changes fastest.
Arguments:
- tokens: bfloat16 [8192, 3584], P('expert', 'dp'), may hold values from -6 to 6
- routes: int32 [8192, 4], P('expert'), may hold values from 0 to 63, all different within a row; in each aligned block of 128 rows (0 to 127, 128 to 255, ...) at most 12 rows name the same one
- gates: float32 [8192, 4], P('expert'), may hold values from 0.1 to 1
- w_gate: bfloat16 [64, 3584, 1024], P('expert', 'dp'), may hold values from -0.09375 to 0.09375
- w_up: bfloat16 [64, 3584, 1024], P('expert', 'dp'), may hold values from -0.09375 to 0.09375
- w_down: bfloat16 [64, 1024, 3584], P('expert', None, 'dp'), may hold values from -0.1875 to 0.1875
- cotangent: bfloat16 [8192, 3584], P('expert', 'dp'), may hold values from -1.5 to 1.5
Outputs:
- mixed: bfloat16 [8192, 3584], P('expert', 'dp')
- token_grad: bfloat16 [8192, 3584], P('expert', 'dp')
- gate_grad: float32 [8192, 4], P('expert')
- w_gate_grad: bfloat16 [64, 3584, 1024], P('expert', 'dp')
- w_up_grad: bfloat16 [64, 3584, 1024], P('expert', 'dp')
- w_down_grad: bfloat16 [64, 1024, 3584], P('expert', None, 'dp')
The draws below stay inside these ranges and needn't reach their ends.
Inputs may be any that keep to these rules, and one draw needn't show every extreme that they name: `routes`: each row names 4 different experts. Within the 128 rows of one index of the expert axis (aligned blocks of rows), no expert is named more than 12 times, and in every draw some expert is named exactly 12 times in some block.
All inputs are finite; a program needn't handle non-finite values.
Results may differ from the reference program's by a relative error of at most 0.028.
Values may be sent and summed in bfloat16 or wider, within the bound.
No kernel may reach another device: no remote copies, remote signals or barrier semaphores. Data moves between devices by JAX's collectives and lax.ppermute only.
A program may use at most 128 MiB of HBM per device.

```python
import math
import jax
import jax.numpy as jnp
import numpy as np
from jax import lax

D = 3584
HIDDEN_SIZE = 1024
TOK_DEV = 128
TOPK = 4
EXPERTS = 64
TOKENS = 8192
CAP = 12
N_DP = 4
N_EXPERT = 64


def block_levels(stream_key, extent, split, low, high):
    def one(dim, shards_of):
        steps = jax.random.uniform(jax.random.fold_in(jax.random.fold_in(stream_key, 6), dim), (shards_of,), jnp.float32, low / len(split), high / len(split))
        return jnp.repeat(jnp.exp(steps), extent[dim] // shards_of).reshape((-1,) + (1,) * (len(extent) - dim - 1))

    gain = one(*split[0])
    for cut in split[1:]:
        gain = gain * one(*cut)
    return gain


def shared_out(key, own, number, rows, number_of, top, most, lean):
    sequence = jax.random.permutation(key, number_of)
    packed, usual = portions_of(number_of, rows * top, most, lean, True), portions_of(number_of, rows * top, most, lean, False)
    places = jnp.arange(number_of)

    def named(lengths, offset_by):
        used = int((lengths > 0).sum())
        fixed = max(1, used // 4)
        shifted = fixed + (places - fixed + offset_by * (used - fixed)) % max(1, number_of - fixed)
        return jnp.zeros((number_of,), jnp.int32).at[sequence[jnp.where(places < fixed, places, shifted)]].set(jnp.asarray(lengths, jnp.int32))

    lengths = jnp.where(number % 4 == 0, named(packed, number // 4), named(usual, number - number // 4 - 1))
    mixed = jax.random.permutation(jax.random.fold_in(own, 3), number_of)
    donor, sink = mixed[0:number_of // 2 * 2:2], mixed[1:number_of // 2 * 2:2]
    slack = jnp.minimum(lengths[donor] - 1, most - lengths[sink]) // 2
    slack = jnp.where((donor == sequence[0]) | (sink == sequence[0]) | (lengths[sink] == 0), 0, jnp.maximum(slack, 0))
    shifted = jax.random.randint(jax.random.fold_in(own, 4), (number_of // 2,), 0, 1 << 20) % (slack + 1)
    lengths = lengths.at[donor].add(-shifted).at[sink].add(shifted)
    items = jnp.searchsorted(jnp.cumsum(lengths), jnp.arange(rows * top), side="right").astype(jnp.int32)
    listing = items.reshape(top, rows).T
    listing = listing[jax.random.permutation(jax.random.fold_in(own, 1), rows)]
    offset_by = jax.random.randint(jax.random.fold_in(own, 2), (rows, 1), 0, top)
    return jnp.take_along_axis(listing, (jnp.arange(top)[None, :] + offset_by) % top, axis=1)


def portions_of(number_of, total, most, skew, full):
    portions = [(1 << 20) // math.isqrt(standing ** skew) + 1 for standing in range(1, number_of + 1)]
    largest = most if full else min(most, max(-(-total // number_of), total * portions[0] // sum(portions)))
    least = 1 if total - largest >= number_of - 1 else 0
    holding, surplus = [largest] + [least] * (number_of - 1), total - largest - least * (number_of - 1)
    while surplus > 0:
        free = [i for i in range(1, number_of) if holding[i] < largest] or [i for i in range(1, number_of) if holding[i] < most]
        whole, budget = sum([portions[i] for i in free]), surplus
        for i in free:
            addition = min(most - holding[i], max(1, budget * portions[i] // whole), surplus)
            holding[i] = holding[i] + addition
            surplus = surplus - addition
    return np.array(holding)


def bell_draw(rng, dims, width, limit, shards=(), kind=jnp.bfloat16):
    drawn = width * jax.random.normal(rng, dims, jnp.float32)
    if shards:
        drawn = drawn * block_levels(rng, dims, shards, -0.22, 0.18)
    return jnp.clip(drawn, -limit, limit).astype(kind)


def setup_inputs(seed: int = 0) -> dict:
    seeds = jax.random.split(jax.random.key(seed), 8)
    tokens = bell_draw(seeds[0], (TOKENS, D), 1.0, 6.0, ((0, 64), (1, 4)))
    routes_keys = jax.random.split(jax.random.fold_in(seeds[1], 1), TOKENS // TOK_DEV)
    routes_turns = jax.random.permutation(jax.random.fold_in(seeds[1], 3), TOKENS // TOK_DEV)
    routes = jax.vmap(lambda own, number: shared_out(jax.random.fold_in(seeds[1], 2), own, number, TOK_DEV, EXPERTS, TOPK, CAP, 2))(routes_keys, routes_turns).reshape((TOKENS, TOPK))
    gates = jnp.clip(jnp.exp(math.log(1.0) - 2.3025851 * jax.random.uniform(seeds[2], (TOKENS, TOPK), jnp.float32) ** block_levels(seeds[2], (TOKENS, TOPK), ((0, 64),), -0.2, 0.2)), 0.1, 1.0)
    w_gate = bell_draw(seeds[3], (EXPERTS, D, HIDDEN_SIZE), D ** -0.5, 0.09375, ((0, 64), (1, 4)))
    w_up = bell_draw(seeds[4], (EXPERTS, D, HIDDEN_SIZE), D ** -0.5, 0.09375, ((0, 64), (1, 4)))
    w_down = bell_draw(seeds[5], (EXPERTS, HIDDEN_SIZE, D), HIDDEN_SIZE ** -0.5, 0.1875, ((0, 64), (2, 4)))
    cotangent = bell_draw(seeds[6], (TOKENS, D), 0.25, 1.5, ((0, 64), (1, 4)))
    return dict(tokens=tokens, routes=routes, gates=gates, w_gate=w_gate, w_up=w_up, w_down=w_down, cotangent=cotangent)


def block_sum(left, right):
    row_count = left.shape[0]
    block_width = left.shape[1] // N_DP
    left_blocks = left.reshape(row_count, N_DP, block_width).astype(jnp.float32)
    right_blocks = right.reshape(N_DP, block_width, right.shape[1]).astype(jnp.float32)
    partials = jnp.einsum('rbd,bdh->brh', left_blocks, right_blocks)
    rounded = lax.optimization_barrier(partials.astype(jnp.bfloat16))
    return lax.optimization_barrier(jnp.sum(rounded.astype(jnp.float32), axis=0))

def full_grad(left, right):
    return jnp.dot(left.T, right, preferred_element_type=jnp.float32).astype(jnp.bfloat16)

def slot_table(routes):
    flat_routes = routes.reshape(N_EXPERT, TOK_DEV * TOPK).astype(jnp.int32)
    labels = jnp.arange(EXPERTS, dtype=jnp.int32)
    onehot = (flat_routes[:, :, None] == labels[None, None, :]).astype(jnp.int32)
    earlier = jnp.cumsum(onehot, axis=1) - onehot
    rank_in = lax.optimization_barrier(jnp.sum(earlier * onehot, axis=2)).astype(jnp.int32)
    source = jnp.arange(N_EXPERT, dtype=jnp.int32)[:, None]
    position = flat_routes * (N_EXPERT * CAP) + source * CAP + rank_in
    pair_ids = jnp.arange(TOKENS * TOPK, dtype=jnp.int32)
    table = jnp.full((EXPERTS * N_EXPERT * CAP,), TOKENS * TOPK, jnp.int32)
    table = table.at[position.reshape(-1)].set(pair_ids)
    return table.reshape(EXPERTS, N_EXPERT * CAP)

def reference(tokens, routes, gates, w_gate, w_up, w_down, cotangent):
    none_row = TOKENS * TOPK
    table = slot_table(routes)
    token_pad = jnp.concatenate([tokens, jnp.zeros((1, D), jnp.bfloat16)], axis=0)
    scaled = (gates[:, :, None] * cotangent.astype(jnp.float32)[:, None, :]).astype(jnp.bfloat16)
    scaled_pad = jnp.concatenate([scaled.reshape(none_row, D), jnp.zeros((1, D), jnp.bfloat16)], axis=0)

    def expert_step(carry, inputs):
        outs_all, grads_all = carry
        slot_rows, gate_weight, up_weight, down_weight = inputs
        token_rows = jnp.where(slot_rows < none_row, slot_rows // TOPK, TOKENS).astype(jnp.int32)
        inputs_rows = token_pad[token_rows]
        cot_rows = scaled_pad[slot_rows]
        gate_pre = block_sum(inputs_rows, gate_weight)
        up_pre = block_sum(inputs_rows, up_weight)
        sigmoid_gate = jax.nn.sigmoid(gate_pre)
        active = gate_pre * sigmoid_gate
        hidden = (active * up_pre).astype(jnp.bfloat16)
        expert_out = jnp.dot(hidden, down_weight, preferred_element_type=jnp.float32).astype(jnp.bfloat16)
        hidden_grad = block_sum(cot_rows, down_weight.T)
        gate_pre_grad = (hidden_grad * up_pre * sigmoid_gate * (1.0 + gate_pre * (1.0 - sigmoid_gate))).astype(jnp.bfloat16)
        up_pre_grad = (hidden_grad * active).astype(jnp.bfloat16)
        pair_grad = (jnp.dot(gate_pre_grad, gate_weight.T, preferred_element_type=jnp.float32) + jnp.dot(up_pre_grad, up_weight.T, preferred_element_type=jnp.float32)).astype(jnp.bfloat16)
        gate_weight_grad = full_grad(inputs_rows, gate_pre_grad)
        up_weight_grad = full_grad(inputs_rows, up_pre_grad)
        down_weight_grad = full_grad(hidden, cot_rows)
        outs_all = outs_all.at[slot_rows].set(expert_out)
        grads_all = grads_all.at[slot_rows].set(pair_grad)
        return ((outs_all, grads_all), (gate_weight_grad, up_weight_grad, down_weight_grad))
    start = (jnp.zeros((none_row + 1, D), jnp.bfloat16), jnp.zeros((none_row + 1, D), jnp.bfloat16))
    (outs_all, grads_all), weight_grads = lax.scan(expert_step, start, (table, w_gate, w_up, w_down))
    expert_out = outs_all[:none_row].reshape(TOKENS, TOPK, D).astype(jnp.float32)
    mixed = lax.optimization_barrier(jnp.sum(gates[:, :, None] * expert_out, axis=1)).astype(jnp.bfloat16)
    gate_grad = lax.optimization_barrier(jnp.sum(expert_out * cotangent.astype(jnp.float32)[:, None, :], axis=2))
    token_grad = lax.optimization_barrier(jnp.sum(grads_all[:none_row].reshape(TOKENS, TOPK, D).astype(jnp.float32), axis=1)).astype(jnp.bfloat16)
    return (mixed, token_grad, gate_grad, weight_grads[0], weight_grads[1], weight_grads[2])
```

```python
import jax
import jax.numpy as jnp
from jax import lax
from jax.experimental import pallas as pl
from jax.experimental.pallas import tpu as pltpu
from jax.sharding import Mesh, PartitionSpec as P

BF = jnp.bfloat16
F32 = jnp.float32
NZ, NXH, NY = 8, 2, 4
PLANE = NXH * NY
TOPK = 4
CAP = 12
TOK = 128
SEG = NZ * CAP
ROWS = PLANE * SEG
QF = 896
HID = 1024
HALF = HID // 2
EXTRA = 8
SWAP = [(0, 1), (1, 0)]
SMALL = pl.CostEstimate(flops=1, bytes_accessed=1, transcendentals=0)


def _any(n):
    return [pl.BlockSpec(memory_space=pl.ANY)] * n


def _ring(step):
    return [(i, (i + step) % NZ) for i in range(NZ)]


def _up(x):
    return lax.ppermute(x, "z", _ring(1))


def _down(x):
    return lax.ppermute(x, "z", _ring(-1))


def gather_ring(x):
    out = [None] * NZ
    out[0] = ahead = behind = x
    for s in range(1, NZ // 2 + 1):
        ahead = _up(ahead)
        out[s] = ahead
        if s < NZ // 2:
            behind = _down(behind)
            out[NZ - s] = behind
    return out


def scatter_ring(parts):
    half = NZ // 2

    def add(a, b):
        return (a.astype(F32) + b.astype(F32)).astype(BF)

    low = _down(parts[half])
    high = _up(parts[half + 1])
    steps = [low, high]
    for s in range(half - 1, 0, -1):
        low = _down(add(low, parts[s]))
        steps.append(low)
        if s > 1:
            high = _up(add(high, parts[NZ - s + 1]))
            steps.append(high)
    return parts[0].astype(F32) + low.astype(F32) + high.astype(F32), steps


def _onehot(pos):
    rows = lax.broadcasted_iota(jnp.int32, (PLANE, SEG, TOK), 1).astype(F32)
    return rows == pos[:, None, :]


def select_tokens_kernel(z_ref, *refs):
    blocks, (rows_ref, pos_ref, gate_ref, route_ref, hot, stack) = refs[:NZ], refs[-6:]
    base = (z_ref[0] * PLANE).astype(F32)
    ids = base + lax.broadcasted_iota(jnp.int32, (PLANE, TOK), 0).astype(F32)
    before = (
        lax.broadcasted_iota(jnp.int32, (TOK, TOK), 0)
        < lax.broadcasted_iota(jnp.int32, (TOK, TOK), 1)
    ).astype(BF)
    for d in range(NZ):
        side = blocks[d][TOK : TOK + EXTRA, :].astype(F32)
        routed = jnp.zeros((PLANE, TOK), F32)
        gate = jnp.zeros((PLANE, TOK), F32)
        for k in range(TOPK):
            match = side[k : k + 1, 0:TOK] == ids
            weight = side[k : k + 1, TOK : 2 * TOK] + side[k : k + 1, 2 * TOK : 3 * TOK]
            routed += match.astype(F32)
            gate += jnp.where(match, weight, 0.0)
        rank = jnp.dot(routed.astype(BF), before, preferred_element_type=F32)
        pos = jnp.where(routed > 0.0, rank + float(d * CAP), -1.0)
        pos_ref[d] = pos
        gate_ref[d] = gate
        route_ref[d] = side[:, 0:TOK]
        hot[:, d * TOK : (d + 1) * TOK] = (
            _onehot(pos).astype(F32).astype(BF).reshape(ROWS, TOK)
        )
        stack[d * TOK : (d + 1) * TOK, :] = blocks[d][0:TOK, :]
    rows_ref[...] = jnp.dot(
        hot[...], stack[...], preferred_element_type=F32
    ).astype(BF)


def select_tokens(z, blocks, after):
    small = jax.ShapeDtypeStruct((NZ, PLANE, TOK), F32)
    return pl.pallas_call(
        select_tokens_kernel,
        out_shape=(jax.ShapeDtypeStruct((ROWS, QF), BF), small, small, small),
        in_specs=[pl.BlockSpec(memory_space=pltpu.SMEM)]
        + [pl.BlockSpec(memory_space=pltpu.VMEM)] * NZ
        + _any(len(after)),
        out_specs=[pl.BlockSpec(memory_space=pltpu.VMEM)] * 4,
        scratch_shapes=[
            pltpu.VMEM((ROWS, NZ * TOK), BF),
            pltpu.VMEM((NZ * TOK, QF), BF),
        ],
        compiler_params=pltpu.CompilerParams(vmem_limit_bytes=40 << 20),
        cost_estimate=SMALL,
    )(z, *blocks, *after)


def select_cotangent_kernel(pos_ref, gate_ref, *refs):
    blocks, (rows_ref, grow_ref, hot, stack) = refs[:NZ], refs[NZ:]
    grow = jnp.zeros((PLANE, SEG, TOK), F32)
    for d in range(NZ):
        mask = _onehot(pos_ref[d])
        grow += jnp.where(mask, gate_ref[d][:, None, :], 0.0)
        hot[:, d * TOK : (d + 1) * TOK] = mask.astype(F32).astype(BF).reshape(ROWS, TOK)
        stack[d * TOK : (d + 1) * TOK, :] = blocks[d][...]
    weight = jnp.sum(grow.reshape(ROWS, TOK), axis=1, keepdims=True)
    grow_ref[...] = weight
    rows = jnp.dot(hot[...], stack[...], preferred_element_type=F32)
    rows_ref[...] = (rows * weight).astype(BF)


def select_cotangent(pos, gate, blocks):
    return pl.pallas_call(
        select_cotangent_kernel,
        out_shape=(
            jax.ShapeDtypeStruct((ROWS, QF), BF),
            jax.ShapeDtypeStruct((ROWS, 1), F32),
        ),
        in_specs=[pl.BlockSpec(memory_space=pltpu.VMEM)] * (2 + NZ),
        out_specs=[pl.BlockSpec(memory_space=pltpu.VMEM)] * 2,
        scratch_shapes=[
            pltpu.VMEM((ROWS, NZ * TOK), BF),
            pltpu.VMEM((NZ * TOK, QF), BF),
        ],
        compiler_params=pltpu.CompilerParams(vmem_limit_bytes=40 << 20),
        cost_estimate=SMALL,
    )(pos, gate, *blocks)


def _onehot_t(pos):
    slot = lax.broadcasted_iota(jnp.int32, (PLANE, ROWS), 1)
    lane = lax.broadcasted_iota(jnp.int32, (PLANE, ROWS), 0)
    spread = (slot // SEG == lane).astype(F32).astype(BF)
    place = lax.dot_general(
        pos.T.astype(BF), spread, (((1,), (0,)), ((), ())), preferred_element_type=F32
    )
    within = lax.broadcasted_iota(jnp.int32, (TOK, ROWS), 1) % SEG
    return (place == within.astype(F32)).astype(F32).astype(BF)


def combine_out_kernel(pos_ref, grow_ref, rows_ref, *refs):
    outs, (scaled,) = refs[:NZ], refs[NZ:]
    scaled[...] = (rows_ref[...].astype(F32) * grow_ref[...]).astype(BF)
    for d in range(NZ):
        outs[d][...] = jnp.dot(
            _onehot_t(pos_ref[d]), scaled[...], preferred_element_type=F32
        ).astype(BF)


def combine_out(pos, grow, rows):
    return pl.pallas_call(
        combine_out_kernel,
        out_shape=[jax.ShapeDtypeStruct((TOK, QF), BF)] * NZ,
        in_specs=[pl.BlockSpec(memory_space=pltpu.VMEM)] * 3,
        out_specs=[pl.BlockSpec(memory_space=pltpu.VMEM)] * NZ,
        scratch_shapes=[pltpu.VMEM((ROWS, QF), BF)],
        compiler_params=pltpu.CompilerParams(vmem_limit_bytes=40 << 20),
        cost_estimate=SMALL,
    )(pos, grow, rows)


def combine_grad_kernel(z_ref, pos_ref, route_ref, rows_ref, *refs):
    outs, body = refs[-NZ - 1 : -1], refs[-1]
    base = (z_ref[0] * PLANE).astype(F32)
    ids = base + lax.broadcasted_iota(jnp.int32, (PLANE, TOK), 0).astype(F32)
    inner = []
    for q in range(PLANE):
        body[q * SEG : (q + 1) * SEG, :] = rows_ref[q, 0:SEG, :]
        tail = rows_ref[q, SEG : SEG + EXTRA, :].astype(F32)
        line = tail[:, 0:TOK] + tail[:, TOK : 2 * TOK]
        inner.append(line.T[0:SEG, 0:1])
    for d in range(NZ):
        pos = pos_ref[d]
        outs[d][0:TOK, :] = jnp.dot(
            _onehot_t(pos), body[...], preferred_element_type=F32
        ).astype(BF)
        slot = lax.broadcasted_iota(jnp.int32, (SEG, TOK), 0).astype(F32)
        found = jnp.concatenate(
            [
                jnp.sum(
                    jnp.where(slot == pos[q : q + 1, :], inner[q], 0.0),
                    axis=0,
                    keepdims=True,
                )
                for q in range(PLANE)
            ],
            axis=0,
        )
        route = route_ref[d]
        lines = [
            jnp.sum(
                jnp.where(route[k : k + 1, :] == ids, found, 0.0), axis=0, keepdims=True
            )
            for k in range(TOPK)
        ]
        grads = jnp.concatenate(
            lines + [jnp.zeros((EXTRA - TOPK, TOK), F32)], axis=0
        )
        high = grads.astype(BF)
        low = (grads - high.astype(F32)).astype(BF)
        outs[d][TOK : TOK + EXTRA, :] = jnp.concatenate(
            [high, low, jnp.zeros((EXTRA, QF - 2 * TOK), BF)], axis=1
        )


def combine_grad(z, pos, route, rows, after):
    return pl.pallas_call(
        combine_grad_kernel,
        out_shape=[jax.ShapeDtypeStruct((TOK + EXTRA, QF), BF)] * NZ,
        in_specs=[pl.BlockSpec(memory_space=pltpu.SMEM)]
        + [pl.BlockSpec(memory_space=pltpu.VMEM)] * 3
        + _any(len(after)),
        out_specs=[pl.BlockSpec(memory_space=pltpu.VMEM)] * NZ,
        scratch_shapes=[pltpu.VMEM((ROWS, QF), BF)],
        compiler_params=pltpu.CompilerParams(vmem_limit_bytes=40 << 20),
        cost_estimate=SMALL,
    )(z, pos, route, rows, *after)


def plane_exchange(x):
    return lax.all_to_all(x, ("xhi", "y"), 0, 0, tiled=True)


TILE = 256
STEPS = HALF // TILE


def project(core, x, w, own, add=None, down=False, after=()):
    n_add = 0 if add is None else 1

    def kernel(core_ref, x_ref, w_ref, *refs):
        out_ref = refs[-1]
        side = 1 if down else 0
        out = lax.dot_general(
            x_ref[...], w_ref[...], (((1,), (side,)), ((), ())), preferred_element_type=F32
        )
        if n_add:
            out = out + refs[0][...].astype(F32)
        out_ref[...] = out.astype(BF)

    def column(j, core_ref):
        half = core_ref[0] if own else 1 - core_ref[0]
        return half * STEPS + j

    if down:
        w_spec = pl.BlockSpec((TILE, QF), lambda j, c: (column(j, c), 0))
    else:
        w_spec = pl.BlockSpec((QF, TILE), lambda j, c: (0, column(j, c)))
    tile = pl.BlockSpec((ROWS, TILE), lambda j, c: (0, j))
    return pl.pallas_call(
        kernel,
        out_shape=jax.ShapeDtypeStruct((ROWS, HALF), BF),
        grid_spec=pltpu.PrefetchScalarGridSpec(
            num_scalar_prefetch=1,
            grid=(STEPS,),
            in_specs=[pl.BlockSpec((ROWS, QF), lambda j, c: (0, 0)), w_spec]
            + [tile] * n_add
            + _any(len(after)),
            out_specs=tile,
        ),
        compiler_params=pltpu.CompilerParams(vmem_limit_bytes=24 << 20),
        cost_estimate=SMALL,
    )(core, x, w, *([] if add is None else [add]), *after)


def expert_output(core, own, other, wd):
    rows = 256

    def kernel(core_ref, a_ref, b_ref, wa_ref, wb_ref, out_ref):
        out = jnp.dot(a_ref[...], wa_ref[...], preferred_element_type=F32)
        out += jnp.dot(b_ref[...], wb_ref[...], preferred_element_type=F32)
        out_ref[...] = out.astype(BF)

    half = pl.BlockSpec((rows, HALF), lambda i, c: (i, 0))
    return pl.pallas_call(
        kernel,
        out_shape=jax.ShapeDtypeStruct((ROWS, QF), BF),
        grid_spec=pltpu.PrefetchScalarGridSpec(
            num_scalar_prefetch=1,
            grid=(ROWS // rows,),
            in_specs=[
                half,
                half,
                pl.BlockSpec((HALF, QF), lambda i, c: (c[0], 0)),
                pl.BlockSpec((HALF, QF), lambda i, c: (1 - c[0], 0)),
            ],
            out_specs=pl.BlockSpec((rows, QF), lambda i, c: (i, 0)),
        ),
        compiler_params=pltpu.CompilerParams(vmem_limit_bytes=24 << 20),
        cost_estimate=SMALL,
    )(core, own, other, wd, wd)


def pair_gradient(core, g_own, g_other, u_own, u_other, wg, wu, inner, inner_other):
    group = 2

    def kernel(core_ref, ga, gb, ua, ub, wga, wgb, wua, wub, inner_ref, rest_ref, out_ref):
        out = jnp.zeros((group * SEG, QF), F32)
        for x, w in ((ga, wga), (gb, wgb), (ua, wua), (ub, wub)):
            out += lax.dot_general(
                x[...], w[...], (((1,), (1,)), ((), ())), preferred_element_type=F32
            )
        out_ref[:, 0:SEG, :] = out.astype(BF).reshape(group, SEG, QF)
        values = inner_ref[...] + rest_ref[...]
        high = values.astype(BF)
        low = (values - high.astype(F32)).astype(BF)
        out_ref[:, SEG : SEG + EXTRA, :] = jnp.concatenate(
            [high, low, jnp.zeros((group, EXTRA, QF - 2 * TOK), BF)], axis=2
        )

    half = pl.BlockSpec((group * SEG, HALF), lambda i, c: (i, 0))
    mine = pl.BlockSpec((QF, HALF), lambda i, c: (0, c[0]))
    theirs = pl.BlockSpec((QF, HALF), lambda i, c: (0, 1 - c[0]))
    return pl.pallas_call(
        kernel,
        out_shape=jax.ShapeDtypeStruct((PLANE, SEG + EXTRA, QF), BF),
        grid_spec=pltpu.PrefetchScalarGridSpec(
            num_scalar_prefetch=1,
            grid=(PLANE // group,),
            in_specs=[half] * 4
            + [mine, theirs, mine, theirs]
            + [pl.BlockSpec((group, EXTRA, TOK), lambda i, c: (i, 0, 0))] * 2,
            out_specs=pl.BlockSpec((group, SEG + EXTRA, QF), lambda i, c: (i, 0, 0)),
        ),
        compiler_params=pltpu.CompilerParams(vmem_limit_bytes=32 << 20),
        cost_estimate=SMALL,
    )(core, g_own, g_other, u_own, u_other, wg, wg, wu, wu, inner, inner_other)


PART = 2 * SEG


def hidden_half(gate_near, gate_far, up_near, up_far):
    def kernel(gn, gf, un, uf, out_ref, gate_ref, up_ref):
        gate = gn[...].astype(F32) + gf[...].astype(F32)
        up = un[...].astype(F32) + uf[...].astype(F32)
        sig = jax.nn.sigmoid(gate)
        active = gate * sig
        out_ref[...] = (active * up).astype(BF)
        gate_ref[...] = (up * sig * (1.0 + gate * (1.0 - sig))).astype(BF)
        up_ref[...] = active.astype(BF)

    tile = pl.BlockSpec((PART, HALF), lambda i: (i, 0))
    return pl.pallas_call(
        kernel,
        out_shape=[jax.ShapeDtypeStruct((ROWS, HALF), BF)] * 3,
        grid=(ROWS // PART,),
        in_specs=[tile] * 4,
        out_specs=[tile] * 3,
        cost_estimate=SMALL,
    )(gate_near, gate_far, up_near, up_far)


def hidden_half_grads(back_near, back_far, hidden, gate_factor, up_factor):
    group = PART // SEG

    def kernel(bn, bf, h_ref, gf_ref, uf_ref, gate_ref, up_ref, inner_ref):
        back = bn[...].astype(F32) + bf[...].astype(F32)
        gate_ref[...] = (back * gf_ref[...].astype(F32)).astype(BF)
        up_ref[...] = (back * uf_ref[...].astype(F32)).astype(BF)
        product = h_ref[...].astype(F32) * back
        high = product.astype(BF)
        low = (product - high.astype(F32)).astype(BF)
        ones = jnp.ones((EXTRA, HALF), BF)
        for g in range(group):
            line = jnp.zeros((EXTRA, SEG), F32)
            for term in (high, low):
                line += lax.dot_general(
                    ones,
                    term[g * SEG : (g + 1) * SEG, :],
                    (((1,), (1,)), ((), ())),
                    preferred_element_type=F32,
                )
            inner_ref[g] = jnp.concatenate(
                [line, jnp.zeros((EXTRA, TOK - SEG), F32)], axis=1
            )

    tile = pl.BlockSpec((PART, HALF), lambda i: (i, 0))
    return pl.pallas_call(
        kernel,
        out_shape=(
            jax.ShapeDtypeStruct((ROWS, HALF), BF),
            jax.ShapeDtypeStruct((ROWS, HALF), BF),
            jax.ShapeDtypeStruct((PLANE, EXTRA, TOK), F32),
        ),
        grid=(ROWS // PART,),
        in_specs=[tile] * 5,
        out_specs=(tile, tile, pl.BlockSpec((group, EXTRA, TOK), lambda i: (i, 0, 0))),
        cost_estimate=SMALL,
    )(back_near, back_far, hidden, gate_factor, up_factor)


def core_swap(x):
    return lax.ppermute(x, "core", SWAP)


def far_swap(x):
    return lax.ppermute(x, "xlo", SWAP)


def whole(core, own, other):
    first = jnp.where(core == 0, own, other)
    second = jnp.where(core == 0, other, own)
    return jnp.concatenate([first, second], axis=1)


def per_device(tokens, routes, gates, w_gate, w_up, w_down, cotangent):
    z = lax.axis_index("z").astype(jnp.int32).reshape(1)
    core = lax.axis_index("core")
    wg, wu, wd = w_gate[0], w_up[0], w_down[0]

    gates_t = gates.T
    high = gates_t.astype(BF)
    low = (gates_t - high.astype(F32)).astype(BF)
    side = jnp.concatenate([routes.T.astype(BF), high, low], axis=1)
    side = jnp.pad(side, ((0, EXTRA - TOPK), (0, QF - 3 * TOK)))
    token_blocks = gather_ring(jnp.concatenate([tokens, side], axis=0))
    cot_blocks = gather_ring(cotangent)
    c1 = core.astype(jnp.int32).reshape(1)

    rows, pos, gate, route = select_tokens(z, token_blocks, cot_blocks[1:])
    inputs = plane_exchange(rows.reshape(PLANE, SEG, QF)).reshape(ROWS, QF)
    crows, grow = select_cotangent(pos, gate, cot_blocks)
    cots = plane_exchange(crows.reshape(PLANE, SEG, QF)).reshape(ROWS, QF)

    g_other = project(c1, inputs, wg, own=False)
    g_recv = core_swap(g_other)
    u_other = project(c1, inputs, wu, own=False, after=(g_other,))
    u_recv = core_swap(u_other)
    g_near = project(c1, inputs, wg, own=True, add=g_recv, after=(u_other,))
    u_near = project(c1, inputs, wu, own=True, add=u_recv, after=(g_near,))
    g_far = far_swap(g_near)
    u_far = far_swap(u_near)

    h_other = project(c1, cots, wd, own=False, down=True, after=(u_near,))
    h_near = project(c1, cots, wd, own=True, down=True, add=core_swap(h_other))
    h_far = far_swap(h_near)

    hidden_own, gate_factor, up_factor = hidden_half(g_near, g_far, u_near, u_far)
    hidden_other = core_swap(hidden_own)
    expert_out = expert_output(c1, hidden_own, hidden_other, wd)
    back_out = plane_exchange(expert_out.reshape(PLANE, SEG, QF)).reshape(ROWS, QF)
    mixed, out_steps = scatter_ring(combine_out(pos, grow, back_out))
    mixed = mixed.astype(BF)

    gpg_own, upg_own, inner = hidden_half_grads(
        h_near, h_far, hidden_own, gate_factor, up_factor
    )
    gpg_other = core_swap(gpg_own)
    upg_other = core_swap(upg_own)
    pair = pair_gradient(c1, gpg_own, gpg_other, upg_own, upg_other, wg, wu, inner, core_swap(inner))
    back_grad = plane_exchange(pair)
    total, _ = scatter_ring(combine_grad(z, pos, route, back_grad, out_steps[:2]))
    token_grad = total[0:TOK].astype(BF)
    gate_sum = total[TOK : TOK + TOPK, 0:TOK] + total[TOK : TOK + TOPK, TOK : 2 * TOK]
    gate_grad = (gate_sum / gates_t).T

    hidden = whole(core, hidden_own, hidden_other)
    gpg = whole(core, gpg_own, gpg_other)
    upg = whole(core, upg_own, upg_other)
    w_gate_grad = jnp.einsum("rq,rh->qh", inputs, gpg, preferred_element_type=F32).astype(BF)
    w_up_grad = jnp.einsum("rq,rh->qh", inputs, upg, preferred_element_type=F32).astype(BF)
    w_down_grad = jnp.einsum("rh,rq->hq", hidden, cots, preferred_element_type=F32).astype(BF)
    return (mixed, token_grad, gate_grad, w_gate_grad[None], w_up_grad[None], w_down_grad[None])


def solution(mesh):
    parts = Mesh(
        mesh.devices.reshape(2, 2, NZ, NXH, NY), ("xlo", "core", "z", "xhi", "y")
    )
    expert, dp = ("z", "xhi", "y"), ("xlo", "core")
    return jax.shard_map(
        per_device,
        mesh=parts,
        in_specs=(
            P(expert, dp),
            P(expert, None),
            P(expert, None),
            P(expert, dp, None),
            P(expert, dp, None),
            P(expert, None, dp),
            P(expert, dp),
        ),
        out_specs=(
            P(expert, dp),
            P(expert, dp),
            P(expert, None),
            P(expert, dp, None),
            P(expert, dp, None),
            P(expert, None, dp),
        ),
        check_vma=False,
    )
```

```python
import jax
import jax.numpy as jnp
from jax import lax
from jax.experimental import pallas as pl
from jax.experimental.pallas import tpu as pltpu
from jax.sharding import Mesh, PartitionSpec as P

BF = jnp.bfloat16
F32 = jnp.float32
NZ, NXH, NY = 8, 2, 4
PLANE = NXH * NY
TOPK = 4
CAP = 12
TOK = 128
SEG = NZ * CAP
ROWS = PLANE * SEG
QF = 896
HID = 1024
HALF = HID // 2
EXTRA = 8
SWAP = [(0, 1), (1, 0)]
SMALL = pl.CostEstimate(flops=1, bytes_accessed=1, transcendentals=0)


def _any(n):
    return [pl.BlockSpec(memory_space=pl.ANY)] * n


def _ring(step):
    return [(i, (i + step) % NZ) for i in range(NZ)]


def _up(x):
    return lax.ppermute(x, "z", _ring(1))


def _down(x):
    return lax.ppermute(x, "z", _ring(-1))


def gather_ring(x):
    out = [None] * NZ
    out[0] = ahead = behind = x
    for s in range(1, NZ // 2 + 1):
        ahead = _up(ahead)
        out[s] = ahead
        if s < NZ // 2:
            behind = _down(behind)
            out[NZ - s] = behind
    return out


def scatter_ring(parts):
    half = NZ // 2

    def add(a, b):
        return (a.astype(F32) + b.astype(F32)).astype(BF)

    low = _down(parts[half])
    high = _up(parts[half + 1])
    steps = [low, high]
    for s in range(half - 1, 0, -1):
        low = _down(add(low, parts[s]))
        steps.append(low)
        if s > 1:
            high = _up(add(high, parts[NZ - s + 1]))
            steps.append(high)
    return parts[0].astype(F32) + low.astype(F32) + high.astype(F32), steps


def _onehot(pos):
    rows = lax.broadcasted_iota(jnp.int32, (PLANE, SEG, TOK), 1).astype(F32)
    return rows == pos[:, None, :]


def select_tokens_kernel(z_ref, *refs):
    blocks, (rows_ref, pos_ref, gate_ref, route_ref, hot, stack) = refs[:NZ], refs[-6:]
    base = (z_ref[0] * PLANE).astype(F32)
    ids = base + lax.broadcasted_iota(jnp.int32, (PLANE, TOK), 0).astype(F32)
    before = (
        lax.broadcasted_iota(jnp.int32, (TOK, TOK), 0)
        < lax.broadcasted_iota(jnp.int32, (TOK, TOK), 1)
    ).astype(BF)
    for d in range(NZ):
        side = blocks[d][TOK : TOK + EXTRA, :].astype(F32)
        routed = jnp.zeros((PLANE, TOK), F32)
        gate = jnp.zeros((PLANE, TOK), F32)
        for k in range(TOPK):
            match = side[k : k + 1, 0:TOK] == ids
            weight = side[k : k + 1, TOK : 2 * TOK] + side[k : k + 1, 2 * TOK : 3 * TOK]
            routed += match.astype(F32)
            gate += jnp.where(match, weight, 0.0)
        rank = jnp.dot(routed.astype(BF), before, preferred_element_type=F32)
        pos = jnp.where(routed > 0.0, rank + float(d * CAP), -1.0)
        pos_ref[d] = pos
        gate_ref[d] = gate
        route_ref[d] = side[:, 0:TOK]
        hot[:, d * TOK : (d + 1) * TOK] = (
            _onehot(pos).astype(F32).astype(BF).reshape(ROWS, TOK)
        )
        stack[d * TOK : (d + 1) * TOK, :] = blocks[d][0:TOK, :]
    rows_ref[...] = jnp.dot(
        hot[...], stack[...], preferred_element_type=F32
    ).astype(BF)


def select_tokens(z, blocks, after):
    small = jax.ShapeDtypeStruct((NZ, PLANE, TOK), F32)
    return pl.pallas_call(
        select_tokens_kernel,
        out_shape=(jax.ShapeDtypeStruct((ROWS, QF), BF), small, small, small),
        in_specs=[pl.BlockSpec(memory_space=pltpu.SMEM)]
        + [pl.BlockSpec(memory_space=pltpu.VMEM)] * NZ
        + _any(len(after)),
        out_specs=[pl.BlockSpec(memory_space=pltpu.VMEM)] * 4,
        scratch_shapes=[
            pltpu.VMEM((ROWS, NZ * TOK), BF),
            pltpu.VMEM((NZ * TOK, QF), BF),
        ],
        compiler_params=pltpu.CompilerParams(vmem_limit_bytes=40 << 20),
        cost_estimate=SMALL,
    )(z, *blocks, *after)


def select_cotangent_kernel(pos_ref, gate_ref, *refs):
    blocks, (rows_ref, grow_ref, hot, stack) = refs[:NZ], refs[NZ:]
    grow = jnp.zeros((PLANE, SEG, TOK), F32)
    for d in range(NZ):
        mask = _onehot(pos_ref[d])
        grow += jnp.where(mask, gate_ref[d][:, None, :], 0.0)
        hot[:, d * TOK : (d + 1) * TOK] = mask.astype(F32).astype(BF).reshape(ROWS, TOK)
        stack[d * TOK : (d + 1) * TOK, :] = blocks[d][...]
    weight = jnp.sum(grow.reshape(ROWS, TOK), axis=1, keepdims=True)
    grow_ref[...] = weight
    rows = jnp.dot(hot[...], stack[...], preferred_element_type=F32)
    rows_ref[...] = (rows * weight).astype(BF)


def select_cotangent(pos, gate, blocks):
    return pl.pallas_call(
        select_cotangent_kernel,
        out_shape=(
            jax.ShapeDtypeStruct((ROWS, QF), BF),
            jax.ShapeDtypeStruct((ROWS, 1), F32),
        ),
        in_specs=[pl.BlockSpec(memory_space=pltpu.VMEM)] * (2 + NZ),
        out_specs=[pl.BlockSpec(memory_space=pltpu.VMEM)] * 2,
        scratch_shapes=[
            pltpu.VMEM((ROWS, NZ * TOK), BF),
            pltpu.VMEM((NZ * TOK, QF), BF),
        ],
        compiler_params=pltpu.CompilerParams(vmem_limit_bytes=40 << 20),
        cost_estimate=SMALL,
    )(pos, gate, *blocks)


def _onehot_t(pos):
    slot = lax.broadcasted_iota(jnp.int32, (PLANE, ROWS), 1)
    lane = lax.broadcasted_iota(jnp.int32, (PLANE, ROWS), 0)
    spread = (slot // SEG == lane).astype(F32).astype(BF)
    place = lax.dot_general(
        pos.T.astype(BF), spread, (((1,), (0,)), ((), ())), preferred_element_type=F32
    )
    within = lax.broadcasted_iota(jnp.int32, (TOK, ROWS), 1) % SEG
    return (place == within.astype(F32)).astype(F32).astype(BF)


def combine_out_kernel(pos_ref, grow_ref, rows_ref, *refs):
    outs, (scaled,) = refs[:NZ], refs[NZ:]
    scaled[...] = (rows_ref[...].astype(F32) * grow_ref[...]).astype(BF)
    for d in range(NZ):
        outs[d][...] = jnp.dot(
            _onehot_t(pos_ref[d]), scaled[...], preferred_element_type=F32
        ).astype(BF)


def combine_out(pos, grow, rows):
    return pl.pallas_call(
        combine_out_kernel,
        out_shape=[jax.ShapeDtypeStruct((TOK, QF), BF)] * NZ,
        in_specs=[pl.BlockSpec(memory_space=pltpu.VMEM)] * 3,
        out_specs=[pl.BlockSpec(memory_space=pltpu.VMEM)] * NZ,
        scratch_shapes=[pltpu.VMEM((ROWS, QF), BF)],
        compiler_params=pltpu.CompilerParams(vmem_limit_bytes=40 << 20),
        cost_estimate=SMALL,
    )(pos, grow, rows)


def combine_grad_kernel(z_ref, pos_ref, route_ref, rows_ref, *refs):
    outs, body = refs[-NZ - 1 : -1], refs[-1]
    base = (z_ref[0] * PLANE).astype(F32)
    ids = base + lax.broadcasted_iota(jnp.int32, (PLANE, TOK), 0).astype(F32)
    inner = []
    for q in range(PLANE):
        body[q * SEG : (q + 1) * SEG, :] = rows_ref[q, 0:SEG, :]
        tail = rows_ref[q, SEG : SEG + EXTRA, :].astype(F32)
        line = tail[:, 0:TOK] + tail[:, TOK : 2 * TOK]
        inner.append(line.T[0:SEG, 0:1])
    for d in range(NZ):
        pos = pos_ref[d]
        outs[d][0:TOK, :] = jnp.dot(
            _onehot_t(pos), body[...], preferred_element_type=F32
        ).astype(BF)
        slot = lax.broadcasted_iota(jnp.int32, (SEG, TOK), 0).astype(F32)
        found = jnp.concatenate(
            [
                jnp.sum(
                    jnp.where(slot == pos[q : q + 1, :], inner[q], 0.0),
                    axis=0,
                    keepdims=True,
                )
                for q in range(PLANE)
            ],
            axis=0,
        )
        route = route_ref[d]
        lines = [
            jnp.sum(
                jnp.where(route[k : k + 1, :] == ids, found, 0.0), axis=0, keepdims=True
            )
            for k in range(TOPK)
        ]
        grads = jnp.concatenate(
            lines + [jnp.zeros((EXTRA - TOPK, TOK), F32)], axis=0
        )
        high = grads.astype(BF)
        low = (grads - high.astype(F32)).astype(BF)
        outs[d][TOK : TOK + EXTRA, :] = jnp.concatenate(
            [high, low, jnp.zeros((EXTRA, QF - 2 * TOK), BF)], axis=1
        )


def combine_grad(z, pos, route, rows, after):
    return pl.pallas_call(
        combine_grad_kernel,
        out_shape=[jax.ShapeDtypeStruct((TOK + EXTRA, QF), BF)] * NZ,
        in_specs=[pl.BlockSpec(memory_space=pltpu.SMEM)]
        + [pl.BlockSpec(memory_space=pltpu.VMEM)] * 3
        + _any(len(after)),
        out_specs=[pl.BlockSpec(memory_space=pltpu.VMEM)] * NZ,
        scratch_shapes=[pltpu.VMEM((ROWS, QF), BF)],
        compiler_params=pltpu.CompilerParams(vmem_limit_bytes=40 << 20),
        cost_estimate=SMALL,
    )(z, pos, route, rows, *after)


def plane_exchange(x):
    return lax.all_to_all(x, ("xhi", "y"), 0, 0, tiled=True)


TILE = 256
STEPS = HALF // TILE


def project(core, x, w, own, add=None, down=False, after=()):
    n_add = 0 if add is None else 1

    def kernel(core_ref, x_ref, w_ref, *refs):
        out_ref = refs[-1]
        side = 1 if down else 0
        out = lax.dot_general(
            x_ref[...], w_ref[...], (((1,), (side,)), ((), ())), preferred_element_type=F32
        )
        if n_add:
            out = out + refs[0][...].astype(F32)
        out_ref[...] = out.astype(BF)

    def column(j, core_ref):
        half = core_ref[0] if own else 1 - core_ref[0]
        return half * STEPS + j

    if down:
        w_spec = pl.BlockSpec((TILE, QF), lambda j, c: (column(j, c), 0))
    else:
        w_spec = pl.BlockSpec((QF, TILE), lambda j, c: (0, column(j, c)))
    tile = pl.BlockSpec((ROWS, TILE), lambda j, c: (0, j))
    return pl.pallas_call(
        kernel,
        out_shape=jax.ShapeDtypeStruct((ROWS, HALF), BF),
        grid_spec=pltpu.PrefetchScalarGridSpec(
            num_scalar_prefetch=1,
            grid=(STEPS,),
            in_specs=[pl.BlockSpec((ROWS, QF), lambda j, c: (0, 0)), w_spec]
            + [tile] * n_add
            + _any(len(after)),
            out_specs=tile,
        ),
        compiler_params=pltpu.CompilerParams(vmem_limit_bytes=24 << 20),
        cost_estimate=SMALL,
    )(core, x, w, *([] if add is None else [add]), *after)


def expert_output(core, own, other, wd):
    rows = 256

    def kernel(core_ref, a_ref, b_ref, wa_ref, wb_ref, out_ref):
        out = jnp.dot(a_ref[...], wa_ref[...], preferred_element_type=F32)
        out += jnp.dot(b_ref[...], wb_ref[...], preferred_element_type=F32)
        out_ref[...] = out.astype(BF)

    half = pl.BlockSpec((rows, HALF), lambda i, c: (i, 0))
    return pl.pallas_call(
        kernel,
        out_shape=jax.ShapeDtypeStruct((ROWS, QF), BF),
        grid_spec=pltpu.PrefetchScalarGridSpec(
            num_scalar_prefetch=1,
            grid=(ROWS // rows,),
            in_specs=[
                half,
                half,
                pl.BlockSpec((HALF, QF), lambda i, c: (c[0], 0)),
                pl.BlockSpec((HALF, QF), lambda i, c: (1 - c[0], 0)),
            ],
            out_specs=pl.BlockSpec((rows, QF), lambda i, c: (i, 0)),
        ),
        compiler_params=pltpu.CompilerParams(vmem_limit_bytes=24 << 20),
        cost_estimate=SMALL,
    )(core, own, other, wd, wd)


def pair_gradient(core, g_own, g_other, u_own, u_other, wg, wu, inner, inner_other):
    group = 2

    def kernel(core_ref, ga, gb, ua, ub, wga, wgb, wua, wub, inner_ref, rest_ref, out_ref):
        out = jnp.zeros((group * SEG, QF), F32)
        for x, w in ((ga, wga), (gb, wgb), (ua, wua), (ub, wub)):
            out += lax.dot_general(
                x[...], w[...], (((1,), (1,)), ((), ())), preferred_element_type=F32
            )
        out_ref[:, 0:SEG, :] = out.astype(BF).reshape(group, SEG, QF)
        values = inner_ref[...] + rest_ref[...]
        high = values.astype(BF)
        low = (values - high.astype(F32)).astype(BF)
        out_ref[:, SEG : SEG + EXTRA, :] = jnp.concatenate(
            [high, low, jnp.zeros((group, EXTRA, QF - 2 * TOK), BF)], axis=2
        )

    half = pl.BlockSpec((group * SEG, HALF), lambda i, c: (i, 0))
    mine = pl.BlockSpec((QF, HALF), lambda i, c: (0, c[0]))
    theirs = pl.BlockSpec((QF, HALF), lambda i, c: (0, 1 - c[0]))
    return pl.pallas_call(
        kernel,
        out_shape=jax.ShapeDtypeStruct((PLANE, SEG + EXTRA, QF), BF),
        grid_spec=pltpu.PrefetchScalarGridSpec(
            num_scalar_prefetch=1,
            grid=(PLANE // group,),
            in_specs=[half] * 4
            + [mine, theirs, mine, theirs]
            + [pl.BlockSpec((group, EXTRA, TOK), lambda i, c: (i, 0, 0))] * 2,
            out_specs=pl.BlockSpec((group, SEG + EXTRA, QF), lambda i, c: (i, 0, 0)),
        ),
        compiler_params=pltpu.CompilerParams(vmem_limit_bytes=32 << 20),
        cost_estimate=SMALL,
    )(core, g_own, g_other, u_own, u_other, wg, wg, wu, wu, inner, inner_other)


PART = 2 * SEG


def hidden_half(gate_near, gate_far, up_near, up_far):
    def kernel(gn, gf, un, uf, out_ref, gate_ref, up_ref):
        gate = gn[...].astype(F32) + gf[...].astype(F32)
        up = un[...].astype(F32) + uf[...].astype(F32)
        sig = jax.nn.sigmoid(gate)
        active = gate * sig
        out_ref[...] = (active * up).astype(BF)
        gate_ref[...] = (up * sig * (1.0 + gate * (1.0 - sig))).astype(BF)
        up_ref[...] = active.astype(BF)

    tile = pl.BlockSpec((PART, HALF), lambda i: (i, 0))
    return pl.pallas_call(
        kernel,
        out_shape=[jax.ShapeDtypeStruct((ROWS, HALF), BF)] * 3,
        grid=(ROWS // PART,),
        in_specs=[tile] * 4,
        out_specs=[tile] * 3,
        cost_estimate=SMALL,
    )(gate_near, gate_far, up_near, up_far)


def hidden_half_grads(back_near, back_far, hidden, gate_factor, up_factor):
    group = PART // SEG

    def kernel(bn, bf, h_ref, gf_ref, uf_ref, gate_ref, up_ref, inner_ref):
        back = bn[...].astype(F32) + bf[...].astype(F32)
        gate_ref[...] = (back * gf_ref[...].astype(F32)).astype(BF)
        up_ref[...] = (back * uf_ref[...].astype(F32)).astype(BF)
        product = h_ref[...].astype(F32) * back
        high = product.astype(BF)
        low = (product - high.astype(F32)).astype(BF)
        ones = jnp.ones((EXTRA, HALF), BF)
        for g in range(group):
            line = jnp.zeros((EXTRA, SEG), F32)
            for term in (high, low):
                line += lax.dot_general(
                    ones,
                    term[g * SEG : (g + 1) * SEG, :],
                    (((1,), (1,)), ((), ())),
                    preferred_element_type=F32,
                )
            inner_ref[g] = jnp.concatenate(
                [line, jnp.zeros((EXTRA, TOK - SEG), F32)], axis=1
            )

    tile = pl.BlockSpec((PART, HALF), lambda i: (i, 0))
    return pl.pallas_call(
        kernel,
        out_shape=(
            jax.ShapeDtypeStruct((ROWS, HALF), BF),
            jax.ShapeDtypeStruct((ROWS, HALF), BF),
            jax.ShapeDtypeStruct((PLANE, EXTRA, TOK), F32),
        ),
        grid=(ROWS // PART,),
        in_specs=[tile] * 5,
        out_specs=(tile, tile, pl.BlockSpec((group, EXTRA, TOK), lambda i: (i, 0, 0))),
        cost_estimate=SMALL,
    )(back_near, back_far, hidden, gate_factor, up_factor)


def core_swap(x):
    return lax.ppermute(x, "core", SWAP)


def far_swap(x):
    return lax.ppermute(x, "xlo", SWAP)


def whole(core, own, other):
    first = jnp.where(core == 0, own, other)
    second = jnp.where(core == 0, other, own)
    return jnp.concatenate([first, second], axis=1)


def per_device(tokens, routes, gates, w_gate, w_up, w_down, cotangent):
    z = lax.axis_index("z").astype(jnp.int32).reshape(1)
    core = lax.axis_index("core")
    wg, wu, wd = w_gate[0], w_up[0], w_down[0]

    gates_t = gates.T
    high = gates_t.astype(BF)
    low = (gates_t - high.astype(F32)).astype(BF)
    side = jnp.concatenate([routes.T.astype(BF), high, low], axis=1)
    side = jnp.pad(side, ((0, EXTRA - TOPK), (0, QF - 3 * TOK)))
    token_blocks = gather_ring(jnp.concatenate([tokens, side], axis=0))
    cot_blocks = gather_ring(cotangent)
    c1 = core.astype(jnp.int32).reshape(1)

    rows, pos, gate, route = select_tokens(z, token_blocks, cot_blocks[1:4] + cot_blocks[5:])
    inputs = plane_exchange(rows.reshape(PLANE, SEG, QF)).reshape(ROWS, QF)
    crows, grow = select_cotangent(pos, gate, cot_blocks)
    cots = plane_exchange(crows.reshape(PLANE, SEG, QF)).reshape(ROWS, QF)

    g_other = project(c1, inputs, wg, own=False, after=(crows,))
    g_recv = core_swap(g_other)
    u_other = project(c1, inputs, wu, own=False, after=(g_other,))
    u_recv = core_swap(u_other)
    g_near = project(c1, inputs, wg, own=True, add=g_recv, after=(u_other,))
    u_near = project(c1, inputs, wu, own=True, add=u_recv, after=(g_near,))
    g_far = far_swap(g_near)
    u_far = far_swap(u_near)

    h_other = project(c1, cots, wd, own=False, down=True, after=(u_near,))
    h_near = project(c1, cots, wd, own=True, down=True, add=core_swap(h_other))
    h_far = far_swap(h_near)

    hidden_own, gate_factor, up_factor = hidden_half(g_near, g_far, u_near, u_far)
    hidden_other = core_swap(hidden_own)
    expert_out = expert_output(c1, hidden_own, hidden_other, wd)
    back_out = plane_exchange(expert_out.reshape(PLANE, SEG, QF)).reshape(ROWS, QF)
    mixed, out_steps = scatter_ring(combine_out(pos, grow, back_out))
    mixed = mixed.astype(BF)

    gpg_own, upg_own, inner = hidden_half_grads(
        h_near, h_far, hidden_own, gate_factor, up_factor
    )
    gpg_other = core_swap(gpg_own)
    upg_other = core_swap(upg_own)
    pair = pair_gradient(c1, gpg_own, gpg_other, upg_own, upg_other, wg, wu, inner, core_swap(inner))
    back_grad = plane_exchange(pair)
    total, _ = scatter_ring(combine_grad(z, pos, route, back_grad, out_steps[:2]))
    token_grad = total[0:TOK].astype(BF)
    gate_sum = total[TOK : TOK + TOPK, 0:TOK] + total[TOK : TOK + TOPK, TOK : 2 * TOK]
    gate_grad = (gate_sum / gates_t).T

    hidden = whole(core, hidden_own, hidden_other)
    gpg = whole(core, gpg_own, gpg_other)
    upg = whole(core, upg_own, upg_other)
    w_gate_grad = jnp.einsum("rq,rh->qh", inputs, gpg, preferred_element_type=F32).astype(BF)
    w_up_grad = jnp.einsum("rq,rh->qh", inputs, upg, preferred_element_type=F32).astype(BF)
    w_down_grad = jnp.einsum("rh,rq->hq", hidden, cots, preferred_element_type=F32).astype(BF)
    return (mixed, token_grad, gate_grad, w_gate_grad[None], w_up_grad[None], w_down_grad[None])


def solution(mesh):
    parts = Mesh(
        mesh.devices.reshape(2, 2, NZ, NXH, NY), ("xlo", "core", "z", "xhi", "y")
    )
    expert, dp = ("z", "xhi", "y"), ("xlo", "core")
    return jax.shard_map(
        per_device,
        mesh=parts,
        in_specs=(
            P(expert, dp),
            P(expert, None),
            P(expert, None),
            P(expert, dp, None),
            P(expert, dp, None),
            P(expert, None, dp),
            P(expert, dp),
        ),
        out_specs=(
            P(expert, dp),
            P(expert, dp),
            P(expert, None),
            P(expert, dp, None),
            P(expert, dp, None),
            P(expert, None, dp),
        ),
        check_vma=False,
    )
```
